32 devices in a mesh: flow: 32 (over z, y, x, core).
Axes of the slice: x: 2, y: 2, z: 4, core: 2. Of those that a mesh axis runs over, the one named last changes fastest.
Arguments:
- forcing: float32 [2, 12, 768, 1024], P(None, None, 'flow'), may hold values from -1000 to 1000
- viscosity: float32 [768, 1024], P('flow'), may hold values from 0.5 to 4
- friction: float32 [768, 1024], P('flow'), may hold values from 1 to 30
- rotation: float32 [768, 1024], P('flow'), may hold values from -2 to 2
- vertical: float32 [11, 768, 1024], P(None, 'flow'), may hold values from 2 to 20
- ice_mask: int32 [768, 1024], P('flow'), may hold values 0 or 1
- grounded: int32 [768, 1024], P('flow'), may hold values 0 or 1
Outputs:
- solution: float32 [2, 12, 768, 1024], P(None, None, 'flow')
- residual: float32 [2, 12, 768, 1024], P(None, None, 'flow')
The draws below stay inside these ranges and needn't reach their ends.
All inputs are finite; a program needn't handle non-finite values. No bound on the sum of `ice_mask` or of `grounded` on one device may be relied on, other than what follows from the above.
Results may differ from the reference program's by a relative error of at most 0.0003.
Values sent between devices are 32-bit elements; how exact they have to be, the bound alone decides.
A program may use at most 192 MiB of HBM per device.

```python
import math
import jax
import jax.numpy as jnp

NY = 1024
L = 12
ITERS = 3
NX = 768


def draw_forcing(key, part):
    noise_key = jax.random.fold_in(key, 11)
    column_key = jax.random.fold_in(key, 12)
    position = jnp.arange(NX, dtype=jnp.float32) / NX
    column_scale = jnp.exp(jax.random.uniform(column_key, (NY,), jnp.float32, 0.0, math.log(10.0)))
    noise_base = jnp.clip(jax.random.normal(noise_key, (2, L, NX, NY), jnp.float32), -5.0, 5.0)
    row_scale = 3.0 ** position
    return 4.0 * noise_base * row_scale[:, None] * column_scale[None, :]


def touch_ends(result, key, least, top_value):
    place = [jax.random.randint(jax.random.fold_in(key, axis), (), 0, length) for axis, length in enumerate(result.shape)]
    longest = result.shape.index(max(result.shape))
    neighbour = place[:longest] + [(place[longest] + 1) % result.shape[longest]] + place[longest + 1:]
    return result.at[tuple(place)].set(least).at[tuple(neighbour)].set(top_value)


def level_of(key, dims, split, smallest, largest):
    def one(dim, parts):
        steps = jax.random.uniform(jax.random.fold_in(jax.random.fold_in(key, 6), dim), (parts,), jnp.float32, smallest / len(split), largest / len(split))
        return jnp.repeat(jnp.exp(steps), dims[dim] // parts).reshape((-1,) + (1,) * (len(dims) - dim - 1))

    level = one(*split[0])
    for cut in split[1:]:
        level = level * one(*cut)
    return level


def setup_inputs(seed: int = 0) -> dict:
    arg_keys = jax.random.split(jax.random.key(seed), 8)
    forcing = draw_forcing(jax.random.fold_in(arg_keys[7], 71), 0)
    viscosity = jnp.clip(jnp.exp(math.log(4.0) - 2.0794415 * jax.random.uniform(arg_keys[1], (NX, NY), jnp.float32) ** level_of(arg_keys[1], (NX, NY), ((0, 32),), -0.2, 0.2)), 0.5, 4.0)
    friction = jnp.clip(jnp.exp(math.log(30.0) - 3.4011974 * jax.random.uniform(arg_keys[2], (NX, NY), jnp.float32) ** level_of(arg_keys[2], (NX, NY), ((0, 32),), -0.2, 0.2)), 1.0, 30.0)
    rotation = jnp.clip(jax.random.uniform(arg_keys[3], (NX, NY), jnp.float32, -2.0, 2.0) * level_of(arg_keys[3], (NX, NY), ((0, 32),), -0.4, 0.0), -2.0, 2.0)
    vertical = jnp.clip(jnp.exp(math.log(20.0) - 2.3025851 * jax.random.uniform(arg_keys[4], (L - 1, NX, NY), jnp.float32) ** level_of(arg_keys[4], (L - 1, NX, NY), ((1, 32),), -0.2, 0.2)), 2.0, 20.0)
    ice_mask = touch_ends((jax.random.randint(arg_keys[5], (NX, NY), 0, 16) < 15).astype(jnp.int32), jax.random.fold_in(arg_keys[5], 1), 0, 1)
    grounded = touch_ends((jax.random.randint(arg_keys[6], (NX, NY), 0, 4) < 3).astype(jnp.int32), jax.random.fold_in(arg_keys[6], 1), 0, 1)
    return {"forcing": forcing, "viscosity": viscosity, "friction": friction, "rotation": rotation, "vertical": vertical, "ice_mask": ice_mask, "grounded": grounded}


epsilon = 1e-06
relaxation = 0.5
reach_weights = (1.0, 0.6, 0.35, 0.2)

def layer_coefs(basal_drag, vertical):
    zero_plane = jnp.zeros_like(vertical[:1])
    upper_coef = jnp.concatenate([vertical, zero_plane], 0)
    lower_coef = jnp.concatenate([zero_plane, vertical], 0)
    bottom = jnp.concatenate([basal_drag[None], jnp.zeros_like(vertical)], 0)
    return (upper_coef, lower_coef, bottom)

def stencil_apply(padded, viscosity, basal_drag, rotation, ice_cover, vertical):
    row_count = padded.shape[2] - 8
    values = padded[:, :, 4:4 + row_count]
    horizontal = jnp.zeros_like(values)
    for order, weight in enumerate(reach_weights):
        offset = order + 1
        forward_cells = padded[:, :, 4 + offset:4 + offset + row_count]
        backward_cells = padded[:, :, 4 - offset:4 - offset + row_count]
        horizontal = horizontal + weight * (2.0 * values - forward_cells - backward_cells)
    padded_cross = jnp.pad(values, ((0, 0), (0, 0), (0, 0), (1, 1)))
    horizontal = horizontal + (2.0 * values - padded_cross[..., 2:] - padded_cross[..., :-2])
    upper_coef, lower_coef, bottom = layer_coefs(basal_drag, vertical)
    diagonal = upper_coef + lower_coef + bottom + relaxation * viscosity
    shifted_up = jnp.concatenate([values[:, 1:], jnp.zeros_like(values[:, :1])], 1)
    shifted_down = jnp.concatenate([jnp.zeros_like(values[:, :1]), values[:, :-1]], 1)
    turned = jnp.stack([values[1], -values[0]])
    stencil = diagonal * values - upper_coef * shifted_up - lower_coef * shifted_down + rotation * turned + viscosity * horizontal
    return jnp.where(ice_cover > 0.5, stencil, values)

def precondition(vector, viscosity, basal_drag, rotation, ice_cover, vertical):
    active = ice_cover > 0.5
    horiz_total = 2.0 * sum(reach_weights) + 2.0
    upper_coef, lower_coef, bottom = layer_coefs(basal_drag, vertical)
    real_part = upper_coef + lower_coef + bottom + relaxation * viscosity + horiz_total * viscosity
    real_part = jnp.where(active, real_part, jnp.ones_like(real_part))
    imag_part = jnp.where(active, rotation, jnp.zeros_like(rotation))
    coupling = jnp.where(active, vertical, jnp.zeros_like(vertical))
    layer_total = vector.shape[1]
    inv_real, inv_imag, carry_former, carry_latter = ([], [], [], [])
    for layer in range(layer_total):
        pivot_real = real_part[layer]
        pivot_imag = imag_part
        source_former = vector[0, layer]
        source_latter = vector[1, layer]
        if layer > 0:
            link = coupling[layer - 1]
            pivot_real = pivot_real - link * link * inv_real[layer - 1]
            pivot_imag = pivot_imag - link * link * inv_imag[layer - 1]
            source_former = source_former + link * carry_former[layer - 1]
            source_latter = source_latter + link * carry_latter[layer - 1]
        inverse_det = 1.0 / (pivot_real * pivot_real + pivot_imag * pivot_imag)
        entry_real = pivot_real * inverse_det
        entry_imag = -pivot_imag * inverse_det
        inv_real.append(entry_real)
        inv_imag.append(entry_imag)
        carry_former.append(entry_real * source_former + entry_imag * source_latter)
        carry_latter.append(entry_real * source_latter - entry_imag * source_former)
    result_former = [None] * layer_total
    result_latter = [None] * layer_total
    result_former[layer_total - 1] = carry_former[layer_total - 1]
    result_latter[layer_total - 1] = carry_latter[layer_total - 1]
    for layer in range(layer_total - 2, -1, -1):
        link = coupling[layer]
        pushed_former = link * result_former[layer + 1]
        pushed_latter = link * result_latter[layer + 1]
        result_former[layer] = carry_former[layer] + inv_real[layer] * pushed_former + inv_imag[layer] * pushed_latter
        result_latter[layer] = carry_latter[layer] + inv_real[layer] * pushed_latter - inv_imag[layer] * pushed_former
    solved = jnp.stack([jnp.stack(result_former), jnp.stack(result_latter)])
    return jnp.where(active, solved, vector)

def least_squares(columns, start):
    count_cols = len(columns)
    givens_rhs = [start] + [start * 0.0 for index in range(count_cols)]
    cosines, sines, upper_cols = ([], [], [])
    for column_index, column_in in enumerate(columns):
        column = list(column_in)
        for row_index in range(column_index):
            rotated_a = cosines[row_index] * column[row_index] + sines[row_index] * column[row_index + 1]
            rotated_b = -sines[row_index] * column[row_index] + cosines[row_index] * column[row_index + 1]
            column[row_index] = rotated_a
            column[row_index + 1] = rotated_b
        radius = jnp.sqrt(column[column_index] * column[column_index] + column[column_index + 1] * column[column_index + 1])
        cosine = column[column_index] / radius
        sine_value = column[column_index + 1] / radius
        column[column_index] = radius
        cosines.append(cosine)
        sines.append(sine_value)
        upper_cols.append(column)
        next_rhs = -sine_value * givens_rhs[column_index]
        givens_rhs[column_index] = cosine * givens_rhs[column_index]
        givens_rhs[column_index + 1] = next_rhs
    factors = [None] * count_cols
    for column_index in range(count_cols - 1, -1, -1):
        accum = givens_rhs[column_index]
        for later in range(column_index + 1, count_cols):
            accum = accum - upper_cols[later][column_index] * factors[later]
        factors[column_index] = accum / upper_cols[column_index][column_index]
    return factors

def operate(values, coefs):
    padded = jnp.pad(values, ((0, 0), (0, 0), (4, 4), (0, 0)))
    return stencil_apply(padded, *coefs)

def reference(forcing, viscosity, friction, rotation, vertical, ice_mask, grounded):
    ice_cover = jnp.where(ice_mask > 0, jnp.ones_like(viscosity), jnp.zeros_like(viscosity))
    basal_drag = jnp.where(grounded > 0, friction, jnp.zeros_like(friction))
    coefs = (viscosity, basal_drag, rotation, ice_cover, vertical)
    load_norm = jnp.sqrt(jnp.sum(forcing * forcing) + epsilon)
    krylov = [forcing / load_norm]
    searches = []
    columns = []
    for iteration in range(ITERS):
        search = precondition(krylov[iteration], *coefs)
        searches.append(search)
        image = operate(search, coefs)
        column = []
        for vector in krylov:
            weight_now = jnp.sum(image * vector)
            image = image - weight_now * vector
            column.append(weight_now)
        new_norm = jnp.sqrt(jnp.sum(image * image) + epsilon)
        column.append(new_norm)
        columns.append(column)
        if iteration + 1 < ITERS:
            krylov.append(image / new_norm)
    factors = least_squares(columns, load_norm)
    solution = factors[0] * searches[0]
    for index in range(1, ITERS):
        solution = solution + factors[index] * searches[index]
    residual = forcing - operate(solution, coefs)
    return (solution, residual)
```

```python
import functools

import jax
import jax.numpy as jnp
from jax import lax
from jax.experimental import pallas as pl
from jax.experimental.pallas import tpu as pltpu
from jax.sharding import PartitionSpec as P

ITERS = 3
epsilon = 1e-06
relaxation = 0.5
reach_weights = (1.0, 0.6, 0.35, 0.2)
REACH = len(reach_weights)
LANES = 128
SUB = 8
MESH = pl.DeviceIdType.MESH
PAIRS = tuple((i, j) for j in range(ITERS + 1) for i in range(j + 1))


def fold(x):
    lead, (rows, cols) = x.shape[:-2], x.shape[-2:]
    x = x.reshape(lead + (rows // SUB, SUB, cols // LANES, LANES))
    return jnp.swapaxes(x, -3, -2).reshape(lead + (rows * cols // LANES, LANES))


def unfold(x, rows, cols):
    lead = x.shape[:-2]
    x = x.reshape(lead + (rows // SUB, cols // LANES, SUB, LANES))
    return jnp.swapaxes(x, -3, -2).reshape(lead + (rows, cols))


def least_squares(columns, start):
    count_cols = len(columns)
    givens_rhs = [start] + [start * 0.0 for index in range(count_cols)]
    cosines, sines, upper_cols = ([], [], [])
    for column_index, column_in in enumerate(columns):
        column = list(column_in)
        for row in range(column_index):
            rotated_a = cosines[row] * column[row] + sines[row] * column[row + 1]
            rotated_b = -sines[row] * column[row] + cosines[row] * column[row + 1]
            column[row] = rotated_a
            column[row + 1] = rotated_b
        radius = jnp.sqrt(
            column[column_index] * column[column_index]
            + column[column_index + 1] * column[column_index + 1]
        )
        cosine = column[column_index] / radius
        sine_value = column[column_index + 1] / radius
        column[column_index] = radius
        cosines.append(cosine)
        sines.append(sine_value)
        upper_cols.append(column)
        next_rhs = -sine_value * givens_rhs[column_index]
        givens_rhs[column_index] = cosine * givens_rhs[column_index]
        givens_rhs[column_index + 1] = next_rhs
    factors = [None] * count_cols
    for column_index in range(count_cols - 1, -1, -1):
        accum = givens_rhs[column_index]
        for later in range(column_index + 1, count_cols):
            accum = accum - upper_cols[later][column_index] * factors[later]
        factors[column_index] = accum / upper_cols[column_index][column_index]
    return factors


def combine(gram):
    def inner(left, right):
        total = None
        for i, a in enumerate(left):
            for j, b in enumerate(right):
                term = a * b * gram[(min(i, j), max(i, j))]
                total = term if total is None else total + term
        return total

    load_norm = jnp.sqrt(gram[(0, 0)] + epsilon)
    krylov = [[1.0 / load_norm]]
    columns = []
    for j in range(ITERS):
        base = krylov[j]
        image = [base[0]]
        for i in range(1, j + 1):
            image.append(base[i] - base[i - 1])
        image.append(-base[j])
        column = []
        for vector in krylov:
            weight = inner(image, vector)
            image = [
                a - weight * vector[i] if i < len(vector) else a
                for i, a in enumerate(image)
            ]
            column.append(weight)
        new_norm = jnp.sqrt(jnp.maximum(inner(image, image), 0.0) + epsilon)
        column.append(new_norm)
        columns.append(column)
        krylov.append([a / new_norm for a in image])
    factors = least_squares(columns, load_norm)
    coefs = []
    for i in range(ITERS):
        total = None
        for j in range(i, ITERS):
            term = factors[j] * krylov[j][i]
            total = term if total is None else total + term
        coefs.append(total)
    rest = [1.0 - coefs[0]]
    for i in range(1, ITERS):
        rest.append(coefs[i - 1] - coefs[i])
    rest.append(coefs[ITERS - 1])
    return coefs, rest


def kernel(
    count, inner_group, rows, layers,
    f_ref, visc_ref, fric_ref, rot_ref, vert_ref, ice_ref, ground_ref,
    sol_ref, res_ref,
    S, B, ER, EI, LK, VN, ACC, SEND1, GOT1, SEND2, GOT2,
    halo_send, halo_recv, one_send, one_recv, two_send, two_recv,
):
    me = lax.axis_index("flow")
    planes = 2 * layers
    outer_group = count // inner_group
    mine_in = lax.rem(me, inner_group)
    mine_out = me // inner_group
    first = me - mine_in

    def inner_peer(d):
        return first + lax.rem(mine_in + d, inner_group)

    def outer_peer(d):
        return lax.rem(mine_out + d, outer_group) * inner_group + mine_in

    has_left = me > 0
    has_right = me < count - 1
    barrier = pltpu.get_barrier_semaphore()
    for d in range(1, inner_group):
        pl.semaphore_signal(barrier, inc=1, device_id=(inner_peer(d),), device_id_type=MESH)
    for d in range(1, outer_group):
        pl.semaphore_signal(barrier, inc=1, device_id=(outer_peer(d),), device_id_type=MESH)

    @pl.when(has_left)
    def _():
        pl.semaphore_signal(barrier, inc=1, device_id=(me - 1,), device_id_type=MESH)

    @pl.when(has_right)
    def _():
        pl.semaphore_signal(barrier, inc=1, device_id=(me + 1,), device_id_type=MESH)

    zero = jnp.zeros((SUB, LANES), jnp.float32)

    @pl.when(me == 0)
    def _():
        for j in range(ITERS):
            S[j, 0:REACH] = jnp.zeros((REACH, planes, SUB, LANES), jnp.float32)

    @pl.when(me == count - 1)
    def _():
        for j in range(ITERS):
            S[j, rows + REACH : rows + 2 * REACH] = jnp.zeros(
                (REACH, planes, SUB, LANES), jnp.float32
            )

    lane = lax.broadcasted_iota(jnp.int32, (SUB, LANES), 1)
    sub = lax.broadcasted_iota(jnp.int32, (SUB, LANES), 0)
    lane_first, lane_last = lane == 0, lane == LANES - 1
    sub_first, sub_last = sub == 0, sub == SUB - 1
    horiz_total = 2.0 * sum(reach_weights) + 2.0

    def at(x):
        return pl.ds((x // SUB) * (SUB * SUB) + lax.rem(x, SUB), SUB, stride=SUB)

    def eliminate(x, k, source, carry):
        former, latter = source
        if k > 0:
            link = LK[x, k - 1]
            former = former + link * carry[0]
            latter = latter + link * carry[1]
        real, imag = ER[x, k], EI[x, k]
        return real * former + imag * latter, real * latter - imag * former

    def substitute(j, x, result):
        former, latter = result
        for k in range(layers - 2, -1, -1):
            link = LK[x, k]
            former, latter = link * former, link * latter
            real, imag = ER[x, k], EI[x, k]
            former, latter = (
                S[j, x + REACH, k] + real * former + imag * latter,
                S[j, x + REACH, layers + k] + real * latter - imag * former,
            )
            S[j, x + REACH, k] = former
            S[j, x + REACH, layers + k] = latter

    def prepare(x):
        here = at(x)
        ice = ice_ref[here, :] > 0
        visc = visc_ref[here, :]
        drag = jnp.where(ground_ref[here, :] > 0, fric_ref[here, :], 0.0)
        imag_part = jnp.where(ice, rot_ref[here, :], 0.0)
        VN[x] = jnp.where(ice, visc, 0.0)
        above = zero
        real = imag = carry = None
        square = zero
        for k in range(layers):
            below = above
            above = vert_ref[k, here, :] if k < layers - 1 else zero
            part = above + below + relaxation * visc + horiz_total * visc
            if k == 0:
                part = part + drag
            pivot_real = jnp.where(ice, part, 1.0)
            pivot_imag = imag_part
            if k > 0:
                link = jnp.where(ice, below, 0.0)
                LK[x, k - 1] = link
                pivot_real = pivot_real - link * link * real
                pivot_imag = pivot_imag - link * link * imag
            inverse = 1.0 / (pivot_real * pivot_real + pivot_imag * pivot_imag)
            real = pivot_real * inverse
            imag = -pivot_imag * inverse
            ER[x, k] = real
            EI[x, k] = imag
            former, latter = f_ref[0, k, here, :], f_ref[1, k, here, :]
            B[0, x, k] = former
            B[0, x, layers + k] = latter
            square = square + (former * former + latter * latter)
            carry = eliminate(x, k, (former, latter), carry)
            S[0, x + REACH, k] = carry[0]
            S[0, x + REACH, layers + k] = carry[1]
        substitute(0, x, carry)
        ACC[0] = ACC[0] + square

    def advance(j, x):
        scale = VN[x]
        carry = None
        sums = [zero] * (j + 2)
        for k in range(layers):
            source = []
            for c in range(2):
                p = c * layers + k
                u = S[j, x + REACH, p]
                left = pltpu.roll(u, 1, 1)
                left = jnp.where(
                    lane_first, jnp.where(sub_first, 0.0, pltpu.roll(left, 1, 0)), left
                )
                right = pltpu.roll(u, LANES - 1, 1)
                right = jnp.where(
                    lane_last, jnp.where(sub_last, 0.0, pltpu.roll(right, SUB - 1, 0)), right
                )
                total = left + right
                for m, weight in enumerate(reach_weights):
                    total = total + weight * (
                        S[j, x + REACH + m + 1, p] + S[j, x + REACH - m - 1, p]
                    )
                b = scale * total
                B[j + 1, x, p] = b
                for i in range(j + 1):
                    sums[i] = sums[i] + b * B[i, x, p]
                sums[j + 1] = sums[j + 1] + b * b
                source.append(b)
            if j + 1 < ITERS:
                carry = eliminate(x, k, source, carry)
                S[j + 1, x + REACH, k] = carry[0]
                S[j + 1, x + REACH, layers + k] = carry[1]
        if j + 1 < ITERS:
            substitute(j + 1, x, carry)
        for i in range(j + 2):
            slot = PAIRS.index((i, j + 1))
            ACC[slot] = ACC[slot] + sums[i]

    def to_left(j, r):
        return pltpu.make_async_remote_copy(
            src_ref=S.at[j, REACH + r],
            dst_ref=S.at[j, REACH + rows + r],
            send_sem=halo_send.at[j, 0, r],
            recv_sem=halo_recv.at[j, 0, r],
            device_id=(me - 1,),
            device_id_type=MESH,
        )

    def to_right(j, r):
        return pltpu.make_async_remote_copy(
            src_ref=S.at[j, rows + r],
            dst_ref=S.at[j, r],
            send_sem=halo_send.at[j, 1, r],
            recv_sem=halo_recv.at[j, 1, r],
            device_id=(me + 1,),
            device_id_type=MESH,
        )

    def edges(j, produce):
        for i in range(REACH):
            low, high = i, REACH - 1 - i
            produce(low)

            @pl.when(has_left)
            def _(low=low):
                to_left(j, low).start()

            produce(rows - REACH + high)

            @pl.when(has_right)
            def _(high=high):
                to_right(j, high).start()

    ACC[...] = jnp.zeros_like(ACC)
    waits = (inner_group - 1) + (outer_group - 1)
    pl.semaphore_wait(
        barrier, waits + has_left.astype(jnp.int32) + has_right.astype(jnp.int32)
    )

    edges(0, prepare)
    pl.loop(REACH, rows - REACH)(prepare)
    for j in range(ITERS):
        pl.loop(REACH, rows - REACH)(functools.partial(advance, j))

        @pl.when(has_right)
        def _(j=j):
            for r in range(REACH):
                to_left(j, r).wait_recv()

        @pl.when(has_left)
        def _(j=j):
            for r in range(REACH):
                to_right(j, r).wait_recv()

        if j + 1 < ITERS:
            edges(j + 1, functools.partial(advance, j))
        else:
            pl.loop(0, REACH)(functools.partial(advance, j))
            pl.loop(rows - REACH, rows)(functools.partial(advance, j))

    SEND1[...] = jnp.zeros_like(SEND1)
    for slot in range(len(PAIRS)):
        SEND1[slot : slot + 1, :] = jnp.sum(ACC[slot], axis=0, keepdims=True)

    def exchange(size, peer, sent, got, send_sem, recv_sem):
        copies = []
        for d in range(1, size):
            copy = pltpu.make_async_remote_copy(
                src_ref=sent,
                dst_ref=got.at[d - 1],
                send_sem=send_sem.at[d - 1],
                recv_sem=recv_sem.at[d - 1],
                device_id=(peer(d),),
                device_id_type=MESH,
            )
            copy.start()
            copies.append(copy)
        for copy in copies:
            copy.wait_recv()
        return copies

    first_copies = exchange(inner_group, inner_peer, SEND1, GOT1, one_send, one_recv)
    total = SEND1[...]
    for d in range(1, inner_group):
        total = total + GOT1[d - 1]
    SEND2[...] = total
    second_copies = exchange(outer_group, outer_peer, SEND2, GOT2, two_send, two_recv)
    for d in range(1, outer_group):
        total = total + GOT2[d - 1]
    total = jnp.sum(total, axis=1, keepdims=True)
    gram = {pair: total[slot : slot + 1, :] for slot, pair in enumerate(PAIRS)}
    coefs, rest = combine(gram)
    coefs = [jnp.broadcast_to(a, (SUB, LANES)) for a in coefs]
    rest = [jnp.broadcast_to(a, (SUB, LANES)) for a in rest]

    def finish(x):
        here = at(x)
        for c in range(2):
            for k in range(layers):
                p = c * layers + k
                value = coefs[0] * S[0, x + REACH, p]
                for i in range(1, ITERS):
                    value = value + coefs[i] * S[i, x + REACH, p]
                sol_ref[c, k, here, :] = value
                value = rest[0] * B[0, x, p]
                for i in range(1, ITERS + 1):
                    value = value + rest[i] * B[i, x, p]
                res_ref[c, k, here, :] = value

    pl.loop(0, rows)(finish)

    for copy in first_copies + second_copies:
        copy.wait_send()
    for j in range(ITERS):

        @pl.when(has_left)
        def _(j=j):
            for r in range(REACH):
                to_left(j, r).wait_send()

        @pl.when(has_right)
        def _(j=j):
            for r in range(REACH):
                to_right(j, r).wait_send()


def body(count, forcing, viscosity, friction, rotation, vertical, ice_mask, grounded):
    comps, layers, rows, cols = forcing.shape
    planes = comps * layers
    inner_group = 8 if count % 8 == 0 else count
    outer_group = count // inner_group
    folded = [fold(a) for a in (forcing, viscosity, friction, rotation, vertical, ice_mask, grounded)]
    shape = jax.ShapeDtypeStruct(folded[0].shape, jnp.float32)
    slots = -(-len(PAIRS) // SUB) * SUB
    f32 = jnp.float32
    outs = pl.pallas_call(
        functools.partial(kernel, count, inner_group, rows, layers),
        out_shape=(shape, shape),
        in_specs=[pl.BlockSpec(memory_space=pltpu.VMEM)] * len(folded),
        out_specs=(pl.BlockSpec(memory_space=pltpu.VMEM),) * 2,
        scratch_shapes=[
            pltpu.VMEM((ITERS, rows + 2 * REACH, planes, SUB, LANES), f32),
            pltpu.VMEM((ITERS + 1, rows, planes, SUB, LANES), f32),
            pltpu.VMEM((rows, layers, SUB, LANES), f32),
            pltpu.VMEM((rows, layers, SUB, LANES), f32),
            pltpu.VMEM((rows, layers - 1, SUB, LANES), f32),
            pltpu.VMEM((rows, SUB, LANES), f32),
            pltpu.VMEM((len(PAIRS), SUB, LANES), f32),
            pltpu.VMEM((slots, LANES), f32),
            pltpu.VMEM((max(inner_group - 1, 1), slots, LANES), f32),
            pltpu.VMEM((slots, LANES), f32),
            pltpu.VMEM((max(outer_group - 1, 1), slots, LANES), f32),
            pltpu.SemaphoreType.DMA((ITERS, 2, REACH)),
            pltpu.SemaphoreType.DMA((ITERS, 2, REACH)),
            pltpu.SemaphoreType.DMA((max(inner_group - 1, 1),)),
            pltpu.SemaphoreType.DMA((max(inner_group - 1, 1),)),
            pltpu.SemaphoreType.DMA((max(outer_group - 1, 1),)),
            pltpu.SemaphoreType.DMA((max(outer_group - 1, 1),)),
        ],
        compiler_params=pltpu.CompilerParams(
            collective_id=0, has_side_effects=True, vmem_limit_bytes=60 * 1024 * 1024
        ),
    )(*folded)
    return tuple(unfold(a, rows, cols) for a in outs)


def solution(mesh):
    return jax.shard_map(
        functools.partial(body, mesh.shape["flow"]),
        mesh=mesh,
        in_specs=(
            P(None, None, "flow", None),
            P("flow", None),
            P("flow", None),
            P("flow", None),
            P(None, "flow", None),
            P("flow", None),
            P("flow", None),
        ),
        out_specs=(P(None, None, "flow", None), P(None, None, "flow", None)),
        check_vma=False,
    )
```

```python
import functools

import jax
import jax.numpy as jnp
from jax import lax
from jax.experimental import pallas as pl
from jax.experimental.pallas import tpu as pltpu
from jax.sharding import PartitionSpec as P

ITERS = 3
epsilon = 1e-06
relaxation = 0.5
reach_weights = (1.0, 0.6, 0.35, 0.2)
REACH = len(reach_weights)
LANES = 128
SUB = 8
VMEM_BYTES = 67043328
MESH = pl.DeviceIdType.MESH
PAIRS = tuple((i, j) for j in range(ITERS + 1) for i in range(j + 1))


def fold(x):
    lead, (rows, cols) = x.shape[:-2], x.shape[-2:]
    x = x.reshape(lead + (rows // SUB, SUB, cols // LANES, LANES))
    return jnp.swapaxes(x, -3, -2).reshape(lead + (rows * cols // LANES, LANES))


def unfold(x, rows, cols):
    lead = x.shape[:-2]
    x = x.reshape(lead + (rows // SUB, cols // LANES, SUB, LANES))
    return jnp.swapaxes(x, -3, -2).reshape(lead + (rows, cols))


def least_squares(columns, start):
    count_cols = len(columns)
    givens_rhs = [start] + [start * 0.0 for index in range(count_cols)]
    cosines, sines, upper_cols = ([], [], [])
    for column_index, column_in in enumerate(columns):
        column = list(column_in)
        for row in range(column_index):
            rotated_a = cosines[row] * column[row] + sines[row] * column[row + 1]
            rotated_b = -sines[row] * column[row] + cosines[row] * column[row + 1]
            column[row] = rotated_a
            column[row + 1] = rotated_b
        radius = jnp.sqrt(
            column[column_index] * column[column_index]
            + column[column_index + 1] * column[column_index + 1]
        )
        cosine = column[column_index] / radius
        sine_value = column[column_index + 1] / radius
        column[column_index] = radius
        cosines.append(cosine)
        sines.append(sine_value)
        upper_cols.append(column)
        next_rhs = -sine_value * givens_rhs[column_index]
        givens_rhs[column_index] = cosine * givens_rhs[column_index]
        givens_rhs[column_index + 1] = next_rhs
    factors = [None] * count_cols
    for column_index in range(count_cols - 1, -1, -1):
        accum = givens_rhs[column_index]
        for later in range(column_index + 1, count_cols):
            accum = accum - upper_cols[later][column_index] * factors[later]
        factors[column_index] = accum / upper_cols[column_index][column_index]
    return factors


def combine(gram):
    def inner(left, right):
        total = None
        for i, a in enumerate(left):
            for j, b in enumerate(right):
                term = a * b * gram[(min(i, j), max(i, j))]
                total = term if total is None else total + term
        return total

    load_norm = jnp.sqrt(gram[(0, 0)] + epsilon)
    krylov = [[1.0 / load_norm]]
    columns = []
    for j in range(ITERS):
        base = krylov[j]
        image = [base[0]]
        for i in range(1, j + 1):
            image.append(base[i] - base[i - 1])
        image.append(-base[j])
        column = []
        for vector in krylov:
            weight = inner(image, vector)
            image = [
                a - weight * vector[i] if i < len(vector) else a
                for i, a in enumerate(image)
            ]
            column.append(weight)
        new_norm = jnp.sqrt(jnp.maximum(inner(image, image), 0.0) + epsilon)
        column.append(new_norm)
        columns.append(column)
        krylov.append([a / new_norm for a in image])
    factors = least_squares(columns, load_norm)
    coefs = []
    for i in range(ITERS):
        total = None
        for j in range(i, ITERS):
            term = factors[j] * krylov[j][i]
            total = term if total is None else total + term
        coefs.append(total)
    rest = [1.0 - coefs[0]]
    for i in range(1, ITERS):
        rest.append(coefs[i - 1] - coefs[i])
    rest.append(coefs[ITERS - 1])
    return coefs, rest


def kernel(
    count, inner_group, rows, layers,
    f_hbm, visc_hbm, fric_hbm, rot_hbm, vert_hbm, ice_hbm, ground_hbm,
    sol_ref, res_ref,
    f_ref, visc_ref, fric_ref, rot_ref, vert_ref, ice_ref, ground_ref,
    S, B, ER, EI, LK, VN, ACC, SEND1, GOT1, SEND2, GOT2,
    load_sem, halo_send, halo_recv, one_send, one_recv, two_send, two_recv,
):
    me = lax.axis_index("flow")
    planes = 2 * layers
    outer_group = count // inner_group
    mine_in = lax.rem(me, inner_group)
    mine_out = me // inner_group
    first = me - mine_in

    def inner_peer(d):
        return first + lax.rem(mine_in + d, inner_group)

    def outer_peer(d):
        return lax.rem(mine_out + d, outer_group) * inner_group + mine_in

    tiles = rows // SUB
    arguments = (
        (f_hbm, f_ref), (visc_hbm, visc_ref), (fric_hbm, fric_ref), (rot_hbm, rot_ref),
        (vert_hbm, vert_ref), (ice_hbm, ice_ref), (ground_hbm, ground_ref),
    )

    def loads(tile):
        part = pl.ds(tile * SUB * SUB, SUB * SUB)
        copies = []
        for slot, (far, near) in enumerate(arguments):
            place = (slice(None),) * (len(near.shape) - 2) + (part,)
            copies.append(
                pltpu.make_async_copy(far.at[place], near.at[place], load_sem.at[tile, slot])
            )
        return copies

    tile_order = [0] + ([tiles - 1] if tiles > 1 else []) + list(range(1, tiles - 1))
    for tile in tile_order:
        for copy in loads(tile):
            copy.start()

    has_left = me > 0
    has_right = me < count - 1
    barrier = pltpu.get_barrier_semaphore()
    for d in range(1, inner_group):
        pl.semaphore_signal(barrier, inc=1, device_id=(inner_peer(d),), device_id_type=MESH)
    for d in range(1, outer_group):
        pl.semaphore_signal(barrier, inc=1, device_id=(outer_peer(d),), device_id_type=MESH)

    @pl.when(has_left)
    def _():
        pl.semaphore_signal(barrier, inc=1, device_id=(me - 1,), device_id_type=MESH)

    @pl.when(has_right)
    def _():
        pl.semaphore_signal(barrier, inc=1, device_id=(me + 1,), device_id_type=MESH)

    zero = jnp.zeros((SUB, LANES), jnp.float32)

    @pl.when(me == 0)
    def _():
        for j in range(ITERS):
            S[j, 0:REACH] = jnp.zeros((REACH, planes, SUB, LANES), jnp.float32)

    @pl.when(me == count - 1)
    def _():
        for j in range(ITERS):
            S[j, rows + REACH : rows + 2 * REACH] = jnp.zeros(
                (REACH, planes, SUB, LANES), jnp.float32
            )

    lane = lax.broadcasted_iota(jnp.int32, (SUB, LANES), 1)
    sub = lax.broadcasted_iota(jnp.int32, (SUB, LANES), 0)
    lane_first, lane_last = lane == 0, lane == LANES - 1
    sub_first, sub_last = sub == 0, sub == SUB - 1
    horiz_total = 2.0 * sum(reach_weights) + 2.0

    def at(x):
        return pl.ds((x // SUB) * (SUB * SUB) + lax.rem(x, SUB), SUB, stride=SUB)

    def eliminate(x, k, source, carry):
        former, latter = source
        if k > 0:
            link = LK[x, k - 1]
            former = former + link * carry[0]
            latter = latter + link * carry[1]
        real, imag = ER[x, k], EI[x, k]
        return real * former + imag * latter, real * latter - imag * former

    def substitute(j, x, result):
        former, latter = result
        for k in range(layers - 2, -1, -1):
            link = LK[x, k]
            former, latter = link * former, link * latter
            real, imag = ER[x, k], EI[x, k]
            former, latter = (
                S[j, x + REACH, k] + real * former + imag * latter,
                S[j, x + REACH, layers + k] + real * latter - imag * former,
            )
            S[j, x + REACH, k] = former
            S[j, x + REACH, layers + k] = latter

    def prepare(x):
        here = at(x)
        ice = ice_ref[here, :] > 0
        visc = visc_ref[here, :]
        drag = jnp.where(ground_ref[here, :] > 0, fric_ref[here, :], 0.0)
        imag_part = jnp.where(ice, rot_ref[here, :], 0.0)
        VN[x] = jnp.where(ice, visc, 0.0)
        above = zero
        real = imag = carry = None
        square = zero
        for k in range(layers):
            below = above
            above = vert_ref[k, here, :] if k < layers - 1 else zero
            part = above + below + relaxation * visc + horiz_total * visc
            if k == 0:
                part = part + drag
            pivot_real = jnp.where(ice, part, 1.0)
            pivot_imag = imag_part
            if k > 0:
                link = jnp.where(ice, below, 0.0)
                LK[x, k - 1] = link
                pivot_real = pivot_real - link * link * real
                pivot_imag = pivot_imag - link * link * imag
            inverse = 1.0 / (pivot_real * pivot_real + pivot_imag * pivot_imag)
            real = pivot_real * inverse
            imag = -pivot_imag * inverse
            ER[x, k] = real
            EI[x, k] = imag
            former, latter = f_ref[0, k, here, :], f_ref[1, k, here, :]
            B[0, x, k] = former
            B[0, x, layers + k] = latter
            square = square + (former * former + latter * latter)
            carry = eliminate(x, k, (former, latter), carry)
            S[0, x + REACH, k] = carry[0]
            S[0, x + REACH, layers + k] = carry[1]
        substitute(0, x, carry)
        ACC[0] = ACC[0] + square

    def advance(j, x):
        scale = VN[x]
        carry = None
        sums = [zero] * (j + 2)
        for k in range(layers):
            source = []
            for c in range(2):
                p = c * layers + k
                u = S[j, x + REACH, p]
                left = pltpu.roll(u, 1, 1)
                left = jnp.where(
                    lane_first, jnp.where(sub_first, 0.0, pltpu.roll(left, 1, 0)), left
                )
                right = pltpu.roll(u, LANES - 1, 1)
                right = jnp.where(
                    lane_last, jnp.where(sub_last, 0.0, pltpu.roll(right, SUB - 1, 0)), right
                )
                total = left + right
                for m, weight in enumerate(reach_weights):
                    total = total + weight * (
                        S[j, x + REACH + m + 1, p] + S[j, x + REACH - m - 1, p]
                    )
                b = scale * total
                B[j + 1, x, p] = b
                for i in range(j + 1):
                    sums[i] = sums[i] + b * B[i, x, p]
                sums[j + 1] = sums[j + 1] + b * b
                source.append(b)
            if j + 1 < ITERS:
                carry = eliminate(x, k, source, carry)
                S[j + 1, x + REACH, k] = carry[0]
                S[j + 1, x + REACH, layers + k] = carry[1]
        if j + 1 < ITERS:
            substitute(j + 1, x, carry)
        for i in range(j + 2):
            slot = PAIRS.index((i, j + 1))
            ACC[slot] = ACC[slot] + sums[i]

    def to_left(j, r):
        return pltpu.make_async_remote_copy(
            src_ref=S.at[j, REACH + r],
            dst_ref=S.at[j, REACH + rows + r],
            send_sem=halo_send.at[j, 0, r],
            recv_sem=halo_recv.at[j, 0, r],
            device_id=(me - 1,),
            device_id_type=MESH,
        )

    def to_right(j, r):
        return pltpu.make_async_remote_copy(
            src_ref=S.at[j, rows + r],
            dst_ref=S.at[j, r],
            send_sem=halo_send.at[j, 1, r],
            recv_sem=halo_recv.at[j, 1, r],
            device_id=(me + 1,),
            device_id_type=MESH,
        )

    waits = (inner_group - 1) + (outer_group - 1)
    waits = waits + has_left.astype(jnp.int32) + has_right.astype(jnp.int32)

    def edges(j, produce, outer_first):
        for i in range(REACH):
            low = i if outer_first else REACH - 1 - i
            high = REACH - 1 - low
            if j > 0 and not outer_first:
                arrive(j - 1, high, low)
            produce(low)
            produce(rows - REACH + high)
            if j == 0 and i == 0:
                pl.semaphore_wait(barrier, waits)
            if j == ITERS:
                continue

            @pl.when(has_left)
            def _(low=low):
                to_left(j, low).start()

            @pl.when(has_right)
            def _(high=high):
                to_right(j, high).start()

    def arrive(j, from_right, from_left):
        @pl.when(has_right)
        def _():
            to_left(j, from_right).wait_recv()

        @pl.when(has_left)
        def _():
            to_right(j, from_left).wait_recv()

    ACC[...] = jnp.zeros_like(ACC)
    for tile in tile_order[:2]:
        for copy in loads(tile):
            copy.wait()
    edges(0, prepare, True)
    for tile in tile_order[2:]:
        for copy in loads(tile):
            copy.wait()
    pl.loop(REACH, rows - REACH)(prepare)
    for j in range(ITERS):
        pl.loop(REACH, rows - REACH)(functools.partial(advance, j))
        outer_first = j % 2 == 1
        if outer_first:
            for r in range(REACH):
                arrive(j, r, r)
        edges(j + 1, functools.partial(advance, j), outer_first)

    SEND1[...] = jnp.zeros_like(SEND1)
    for slot in range(len(PAIRS)):
        SEND1[slot : slot + 1, :] = jnp.sum(ACC[slot], axis=0, keepdims=True)

    def exchange(size, peer, sent, got, send_sem, recv_sem):
        copies = []
        for d in range(1, size):
            copy = pltpu.make_async_remote_copy(
                src_ref=sent,
                dst_ref=got.at[d - 1],
                send_sem=send_sem.at[d - 1],
                recv_sem=recv_sem.at[d - 1],
                device_id=(peer(d),),
                device_id_type=MESH,
            )
            copy.start()
            copies.append(copy)
        for copy in copies:
            copy.wait_recv()
        return copies

    first_copies = exchange(inner_group, inner_peer, SEND1, GOT1, one_send, one_recv)
    total = SEND1[...]
    for d in range(1, inner_group):
        total = total + GOT1[d - 1]
    SEND2[...] = total
    second_copies = exchange(outer_group, outer_peer, SEND2, GOT2, two_send, two_recv)
    for d in range(1, outer_group):
        total = total + GOT2[d - 1]
    total = jnp.sum(total, axis=1, keepdims=True)
    gram = {pair: total[slot : slot + 1, :] for slot, pair in enumerate(PAIRS)}
    coefs, rest = combine(gram)
    coefs = [jnp.broadcast_to(a, (SUB, LANES)) for a in coefs]
    rest = [jnp.broadcast_to(a, (SUB, LANES)) for a in rest]

    def finish(x):
        here = at(x)
        for c in range(2):
            for k in range(layers):
                p = c * layers + k
                value = coefs[0] * S[0, x + REACH, p]
                for i in range(1, ITERS):
                    value = value + coefs[i] * S[i, x + REACH, p]
                sol_ref[c, k, here, :] = value
                value = rest[0] * B[0, x, p]
                for i in range(1, ITERS + 1):
                    value = value + rest[i] * B[i, x, p]
                res_ref[c, k, here, :] = value

    pl.loop(0, rows)(finish)

    for copy in first_copies + second_copies:
        copy.wait_send()
    for j in range(ITERS):

        @pl.when(has_left)
        def _(j=j):
            for r in range(REACH):
                to_left(j, r).wait_send()

        @pl.when(has_right)
        def _(j=j):
            for r in range(REACH):
                to_right(j, r).wait_send()


def body(count, forcing, viscosity, friction, rotation, vertical, ice_mask, grounded):
    comps, layers, rows, cols = forcing.shape
    planes = comps * layers
    inner_group = 8 if count % 8 == 0 else count
    outer_group = count // inner_group
    folded = [fold(a) for a in (forcing, viscosity, friction, rotation, vertical, ice_mask, grounded)]
    shape = pltpu.VMEM(folded[0].shape, jnp.float32)
    slots = -(-len(PAIRS) // SUB) * SUB
    f32 = jnp.float32
    room = 2 * 4 * forcing.size + 65536
    outs = pl.pallas_call(
        functools.partial(kernel, count, inner_group, rows, layers),
        out_shape=(shape, shape),
        in_specs=[pl.BlockSpec(memory_space=pltpu.HBM)] * len(folded),
        out_specs=(pl.BlockSpec(memory_space=pltpu.VMEM),) * 2,
        scratch_shapes=[pltpu.VMEM(a.shape, a.dtype) for a in folded]
        + [
            pltpu.VMEM((ITERS, rows + 2 * REACH, planes, SUB, LANES), f32),
            pltpu.VMEM((ITERS + 1, rows, planes, SUB, LANES), f32),
            pltpu.VMEM((rows, layers, SUB, LANES), f32),
            pltpu.VMEM((rows, layers, SUB, LANES), f32),
            pltpu.VMEM((rows, layers - 1, SUB, LANES), f32),
            pltpu.VMEM((rows, SUB, LANES), f32),
            pltpu.VMEM((len(PAIRS), SUB, LANES), f32),
            pltpu.VMEM((slots, LANES), f32),
            pltpu.VMEM((max(inner_group - 1, 1), slots, LANES), f32),
            pltpu.VMEM((slots, LANES), f32),
            pltpu.VMEM((max(outer_group - 1, 1), slots, LANES), f32),
            pltpu.SemaphoreType.DMA((rows // SUB, len(folded))),
            pltpu.SemaphoreType.DMA((ITERS, 2, REACH)),
            pltpu.SemaphoreType.DMA((ITERS, 2, REACH)),
            pltpu.SemaphoreType.DMA((max(inner_group - 1, 1),)),
            pltpu.SemaphoreType.DMA((max(inner_group - 1, 1),)),
            pltpu.SemaphoreType.DMA((max(outer_group - 1, 1),)),
            pltpu.SemaphoreType.DMA((max(outer_group - 1, 1),)),
        ],
        compiler_params=pltpu.CompilerParams(
            collective_id=0, has_side_effects=True, vmem_limit_bytes=VMEM_BYTES - room
        ),
    )(*folded)
    return tuple(unfold(a, rows, cols) for a in outs)


def solution(mesh):
    return jax.shard_map(
        functools.partial(body, mesh.shape["flow"]),
        mesh=mesh,
        in_specs=(
            P(None, None, "flow", None),
            P("flow", None),
            P("flow", None),
            P("flow", None),
            P(None, "flow", None),
            P("flow", None),
            P("flow", None),
        ),
        out_specs=(P(None, None, "flow", None), P(None, None, "flow", None)),
        check_vma=False,
    )
```

```python
import functools

import jax
import jax.numpy as jnp
from jax import lax
from jax.experimental import pallas as pl
from jax.experimental.pallas import tpu as pltpu
from jax.sharding import PartitionSpec as P

ITERS = 3
epsilon = 1e-06
relaxation = 0.5
reach_weights = (1.0, 0.6, 0.35, 0.2)
REACH = len(reach_weights)
LANES = 128
SUB = 8
VMEM_BYTES = 67043328
MESH = pl.DeviceIdType.MESH
PAIRS = tuple((i, j) for j in range(ITERS + 1) for i in range(j + 1))


def fold(x):
    lead, (rows, cols) = x.shape[:-2], x.shape[-2:]
    x = x.reshape(lead + (rows // SUB, SUB, cols // LANES, LANES))
    return jnp.swapaxes(x, -3, -2).reshape(lead + (rows * cols // LANES, LANES))


def unfold(x, rows, cols):
    lead = x.shape[:-2]
    x = x.reshape(lead + (rows // SUB, cols // LANES, SUB, LANES))
    return jnp.swapaxes(x, -3, -2).reshape(lead + (rows, cols))


def least_squares(columns, start):
    count_cols = len(columns)
    givens_rhs = [start] + [start * 0.0 for index in range(count_cols)]
    cosines, sines, upper_cols = ([], [], [])
    for column_index, column_in in enumerate(columns):
        column = list(column_in)
        for row in range(column_index):
            rotated_a = cosines[row] * column[row] + sines[row] * column[row + 1]
            rotated_b = -sines[row] * column[row] + cosines[row] * column[row + 1]
            column[row] = rotated_a
            column[row + 1] = rotated_b
        radius = jnp.sqrt(
            column[column_index] * column[column_index]
            + column[column_index + 1] * column[column_index + 1]
        )
        cosine = column[column_index] / radius
        sine_value = column[column_index + 1] / radius
        column[column_index] = radius
        cosines.append(cosine)
        sines.append(sine_value)
        upper_cols.append(column)
        next_rhs = -sine_value * givens_rhs[column_index]
        givens_rhs[column_index] = cosine * givens_rhs[column_index]
        givens_rhs[column_index + 1] = next_rhs
    factors = [None] * count_cols
    for column_index in range(count_cols - 1, -1, -1):
        accum = givens_rhs[column_index]
        for later in range(column_index + 1, count_cols):
            accum = accum - upper_cols[later][column_index] * factors[later]
        factors[column_index] = accum / upper_cols[column_index][column_index]
    return factors


def combine(gram):
    def inner(left, right):
        total = None
        for i, a in enumerate(left):
            for j, b in enumerate(right):
                term = a * b * gram[(min(i, j), max(i, j))]
                total = term if total is None else total + term
        return total

    load_norm = jnp.sqrt(gram[(0, 0)] + epsilon)
    krylov = [[1.0 / load_norm]]
    columns = []
    for j in range(ITERS):
        base = krylov[j]
        image = [base[0]]
        for i in range(1, j + 1):
            image.append(base[i] - base[i - 1])
        image.append(-base[j])
        column = []
        for vector in krylov:
            weight = inner(image, vector)
            image = [
                a - weight * vector[i] if i < len(vector) else a
                for i, a in enumerate(image)
            ]
            column.append(weight)
        new_norm = jnp.sqrt(jnp.maximum(inner(image, image), 0.0) + epsilon)
        column.append(new_norm)
        columns.append(column)
        krylov.append([a / new_norm for a in image])
    factors = least_squares(columns, load_norm)
    coefs = []
    for i in range(ITERS):
        total = None
        for j in range(i, ITERS):
            term = factors[j] * krylov[j][i]
            total = term if total is None else total + term
        coefs.append(total)
    rest = [1.0 - coefs[0]]
    for i in range(1, ITERS):
        rest.append(coefs[i - 1] - coefs[i])
    rest.append(coefs[ITERS - 1])
    return coefs, rest


def kernel(
    count, inner_group, rows, layers,
    f_hbm, visc_hbm, fric_hbm, rot_hbm, vert_hbm, ice_hbm, ground_hbm,
    sol_ref, res_ref,
    f_ref, visc_ref, fric_ref, rot_ref, vert_ref, ice_ref, ground_ref,
    S0, S1, S2, B0, B1, B2, B3, ER, EI, LK, VN, ACC, SEND1, GOT1, SEND2, GOT2,
    load_sem, halo_send, halo_recv, one_send, one_recv, two_send, two_recv,
):
    me = lax.axis_index("flow")
    S, B = (S0, S1, S2), (B0, B1, B2, B3)
    planes = 2 * layers
    outer_group = count // inner_group
    mine_in = lax.rem(me, inner_group)
    mine_out = me // inner_group
    first = me - mine_in

    def inner_peer(d):
        return first + lax.rem(mine_in + d, inner_group)

    def outer_peer(d):
        return lax.rem(mine_out + d, outer_group) * inner_group + mine_in

    tiles = rows // SUB
    arguments = (
        (f_hbm, f_ref), (visc_hbm, visc_ref), (fric_hbm, fric_ref), (rot_hbm, rot_ref),
        (vert_hbm, vert_ref), (ice_hbm, ice_ref), (ground_hbm, ground_ref),
    )

    def loads(tile):
        part = pl.ds(tile * SUB * SUB, SUB * SUB)
        copies = []
        for slot, (far, near) in enumerate(arguments):
            place = (slice(None),) * (len(near.shape) - 2) + (part,)
            copies.append(
                pltpu.make_async_copy(far.at[place], near.at[place], load_sem.at[tile, slot])
            )
        return copies

    tile_order = [0] + ([tiles - 1] if tiles > 1 else []) + list(range(1, tiles - 1))
    for tile in tile_order:
        for copy in loads(tile):
            copy.start()

    has_left = me > 0
    has_right = me < count - 1
    barrier = pltpu.get_barrier_semaphore()
    for d in range(1, inner_group):
        pl.semaphore_signal(barrier, inc=1, device_id=(inner_peer(d),), device_id_type=MESH)
    for d in range(1, outer_group):
        pl.semaphore_signal(barrier, inc=1, device_id=(outer_peer(d),), device_id_type=MESH)

    @pl.when(has_left)
    def _():
        pl.semaphore_signal(barrier, inc=1, device_id=(me - 1,), device_id_type=MESH)

    @pl.when(has_right)
    def _():
        pl.semaphore_signal(barrier, inc=1, device_id=(me + 1,), device_id_type=MESH)

    zero = jnp.zeros((SUB, LANES), jnp.float32)

    @pl.when(me == 0)
    def _():
        for j in range(ITERS):
            S[j][0:REACH] = jnp.zeros((REACH, planes, SUB, LANES), jnp.float32)

    @pl.when(me == count - 1)
    def _():
        for j in range(ITERS):
            S[j][rows + REACH : rows + 2 * REACH] = jnp.zeros(
                (REACH, planes, SUB, LANES), jnp.float32
            )

    lane = lax.broadcasted_iota(jnp.int32, (SUB, LANES), 1)
    sub = lax.broadcasted_iota(jnp.int32, (SUB, LANES), 0)
    lane_first, lane_last = lane == 0, lane == LANES - 1
    sub_first, sub_last = sub == 0, sub == SUB - 1
    horiz_total = 2.0 * sum(reach_weights) + 2.0

    def at(x):
        return pl.ds((x // SUB) * (SUB * SUB) + lax.rem(x, SUB), SUB, stride=SUB)

    def eliminate(x, k, source, carry):
        former, latter = source
        if k > 0:
            link = LK[x, k - 1]
            former = former + link * carry[0]
            latter = latter + link * carry[1]
        real, imag = ER[x, k], EI[x, k]
        return real * former + imag * latter, real * latter - imag * former

    def substitute(j, xs, results):
        for k in range(layers - 2, -1, -1):
            for n, x in enumerate(xs):
                former, latter = results[n]
                link = LK[x, k]
                former, latter = link * former, link * latter
                real, imag = ER[x, k], EI[x, k]
                former, latter = (
                    S[j][x + REACH, k] + real * former + imag * latter,
                    S[j][x + REACH, layers + k] + real * latter - imag * former,
                )
                S[j][x + REACH, k] = former
                S[j][x + REACH, layers + k] = latter
                results[n] = former, latter

    def prepare(*xs):
        count_rows = len(xs)
        places = [at(x) for x in xs]
        ices = [ice_ref[here, :] > 0 for here in places]
        viscs = [visc_ref[here, :] for here in places]
        imag_parts = [
            jnp.where(ice, rot_ref[here, :], 0.0) for ice, here in zip(ices, places)
        ]
        for x, ice, visc in zip(xs, ices, viscs):
            VN[x] = jnp.where(ice, visc, 0.0)
        above = [zero] * count_rows
        inv = [None] * count_rows
        carry = [None] * count_rows
        square = [zero] * count_rows
        for k in range(layers):
            for n, x in enumerate(xs):
                here, ice, visc = places[n], ices[n], viscs[n]
                below = above[n]
                above[n] = vert_ref[k, here, :] if k < layers - 1 else zero
                part = above[n] + below + relaxation * visc + horiz_total * visc
                if k == 0:
                    part = part + jnp.where(ground_ref[here, :] > 0, fric_ref[here, :], 0.0)
                pivot_real = jnp.where(ice, part, 1.0)
                pivot_imag = imag_parts[n]
                if k > 0:
                    link = jnp.where(ice, below, 0.0)
                    LK[x, k - 1] = link
                    pivot_real = pivot_real - link * link * inv[n][0]
                    pivot_imag = pivot_imag - link * link * inv[n][1]
                inverse = 1.0 / (pivot_real * pivot_real + pivot_imag * pivot_imag)
                inv[n] = pivot_real * inverse, -pivot_imag * inverse
                ER[x, k], EI[x, k] = inv[n]
                former, latter = f_ref[0, k, here, :], f_ref[1, k, here, :]
                B[0][x, k] = former
                B[0][x, layers + k] = latter
                square[n] = square[n] + (former * former + latter * latter)
                carry[n] = eliminate(x, k, (former, latter), carry[n])
                S[0][x + REACH, k], S[0][x + REACH, layers + k] = carry[n]
        substitute(0, xs, carry)
        ACC[0] = ACC[0] + sum(square[1:], square[0])

    def advance(j, *xs, close=False):
        scales = [VN[x] for x in xs]
        carry = [None] * len(xs)
        sums = [[zero] * (j + 2) for x in xs]
        for k in range(layers):
            source = [[] for x in xs]
            for c in range(2):
                p = c * layers + k
                seen = {}

                def row(n, offset):
                    key = ("all", n + offset) if close else (n, offset)
                    if key not in seen:
                        start = xs[0] + n if close else xs[n]
                        seen[key] = S[j][start + REACH + offset, p]
                    return seen[key]

                for n, x in enumerate(xs):
                    u = row(n, 0)
                    left = pltpu.roll(u, 1, 1)
                    left = jnp.where(
                        lane_first, jnp.where(sub_first, 0.0, pltpu.roll(left, 1, 0)), left
                    )
                    right = pltpu.roll(u, LANES - 1, 1)
                    right = jnp.where(
                        lane_last, jnp.where(sub_last, 0.0, pltpu.roll(right, SUB - 1, 0)), right
                    )
                    total = left + right
                    for m, weight in enumerate(reach_weights):
                        total = total + weight * (row(n, m + 1) + row(n, -m - 1))
                    b = scales[n] * total
                    B[j + 1][x, p] = b
                    for i in range(j + 1):
                        sums[n][i] = sums[n][i] + b * B[i][x, p]
                    sums[n][j + 1] = sums[n][j + 1] + b * b
                    source[n].append(b)
            if j + 1 < ITERS:
                for n, x in enumerate(xs):
                    carry[n] = eliminate(x, k, source[n], carry[n])
                    S[j + 1][x + REACH, k], S[j + 1][x + REACH, layers + k] = carry[n]
        if j + 1 < ITERS:
            substitute(j + 1, xs, carry)
        for i in range(j + 2):
            slot = PAIRS.index((i, j + 1))
            ACC[slot] = ACC[slot] + sum((a[i] for a in sums[1:]), sums[0][i])

    def to_left(j, r):
        return pltpu.make_async_remote_copy(
            src_ref=S[j].at[REACH + r],
            dst_ref=S[j].at[REACH + rows + r],
            send_sem=halo_send.at[j, 0, r],
            recv_sem=halo_recv.at[j, 0, r],
            device_id=(me - 1,),
            device_id_type=MESH,
        )

    def to_right(j, r):
        return pltpu.make_async_remote_copy(
            src_ref=S[j].at[rows + r],
            dst_ref=S[j].at[r],
            send_sem=halo_send.at[j, 1, r],
            recv_sem=halo_recv.at[j, 1, r],
            device_id=(me + 1,),
            device_id_type=MESH,
        )

    waits = (inner_group - 1) + (outer_group - 1)
    waits = waits + has_left.astype(jnp.int32) + has_right.astype(jnp.int32)

    def edges(j, produce, outer_first):
        for i in range(REACH):
            low = i if outer_first else REACH - 1 - i
            high = REACH - 1 - low
            if j > 0 and not outer_first:
                arrive(j - 1, high, low)
            produce(low, rows - REACH + high)
            if j == 0 and i == 0:
                pl.semaphore_wait(barrier, waits)
            if j == ITERS:
                continue

            @pl.when(has_left)
            def _(low=low):
                to_left(j, low).start()

            @pl.when(has_right)
            def _(high=high):
                to_right(j, high).start()

    def arrive(j, from_right, from_left):
        @pl.when(has_right)
        def _():
            to_left(j, from_right).wait_recv()

        @pl.when(has_left)
        def _():
            to_right(j, from_left).wait_recv()

    ACC[...] = jnp.zeros_like(ACC)
    for tile in tile_order[:2]:
        for copy in loads(tile):
            copy.wait()
    edges(0, prepare, True)
    for tile in tile_order[2:]:
        for copy in loads(tile):
            copy.wait()
    pl.loop(REACH, rows - REACH)(prepare)
    for j in range(ITERS):
        pl.loop(REACH, rows - REACH)(functools.partial(advance, j))
        outer_first = j % 2 == 1
        if outer_first:
            for r in range(REACH):
                arrive(j, r, r)
        edges(j + 1, functools.partial(advance, j), outer_first)

    SEND1[...] = jnp.zeros_like(SEND1)
    for slot in range(len(PAIRS)):
        SEND1[slot : slot + 1, :] = jnp.sum(ACC[slot], axis=0, keepdims=True)

    def exchange(size, peer, sent, got, send_sem, recv_sem):
        copies = []
        for d in range(1, size):
            copy = pltpu.make_async_remote_copy(
                src_ref=sent,
                dst_ref=got.at[d - 1],
                send_sem=send_sem.at[d - 1],
                recv_sem=recv_sem.at[d - 1],
                device_id=(peer(d),),
                device_id_type=MESH,
            )
            copy.start()
            copies.append(copy)
        for copy in copies:
            copy.wait_recv()
        return copies

    first_copies = exchange(inner_group, inner_peer, SEND1, GOT1, one_send, one_recv)
    total = SEND1[...]
    for d in range(1, inner_group):
        total = total + GOT1[d - 1]
    SEND2[...] = total
    second_copies = exchange(outer_group, outer_peer, SEND2, GOT2, two_send, two_recv)
    for d in range(1, outer_group):
        total = total + GOT2[d - 1]
    total = jnp.sum(total, axis=1, keepdims=True)
    gram = {pair: total[slot : slot + 1, :] for slot, pair in enumerate(PAIRS)}
    coefs, rest = combine(gram)
    coefs = [jnp.broadcast_to(a, (SUB, LANES)) for a in coefs]
    rest = [jnp.broadcast_to(a, (SUB, LANES)) for a in rest]

    def finish(x):
        here = at(x)
        for c in range(2):
            for k in range(layers):
                p = c * layers + k
                value = coefs[0] * S[0][x + REACH, p]
                for i in range(1, ITERS):
                    value = value + coefs[i] * S[i][x + REACH, p]
                sol_ref[c, k, here, :] = value
                value = rest[0] * B[0][x, p]
                for i in range(1, ITERS + 1):
                    value = value + rest[i] * B[i][x, p]
                res_ref[c, k, here, :] = value

    pl.loop(0, rows)(finish)

    for copy in first_copies + second_copies:
        copy.wait_send()
    for j in range(ITERS):

        @pl.when(has_left)
        def _(j=j):
            for r in range(REACH):
                to_left(j, r).wait_send()

        @pl.when(has_right)
        def _(j=j):
            for r in range(REACH):
                to_right(j, r).wait_send()


def body(count, forcing, viscosity, friction, rotation, vertical, ice_mask, grounded):
    comps, layers, rows, cols = forcing.shape
    planes = comps * layers
    inner_group = 8 if count % 8 == 0 else count
    outer_group = count // inner_group
    folded = [fold(a) for a in (forcing, viscosity, friction, rotation, vertical, ice_mask, grounded)]
    shape = pltpu.VMEM(folded[0].shape, jnp.float32)
    slots = -(-len(PAIRS) // SUB) * SUB
    f32 = jnp.float32
    room = 2 * 4 * forcing.size + 65536
    outs = pl.pallas_call(
        functools.partial(kernel, count, inner_group, rows, layers),
        out_shape=(shape, shape),
        in_specs=[pl.BlockSpec(memory_space=pltpu.HBM)] * len(folded),
        out_specs=(pl.BlockSpec(memory_space=pltpu.VMEM),) * 2,
        scratch_shapes=[pltpu.VMEM(a.shape, a.dtype) for a in folded]
        + [
            *[pltpu.VMEM((rows + 2 * REACH, planes, SUB, LANES), f32)] * ITERS,
            *[pltpu.VMEM((rows, planes, SUB, LANES), f32)] * (ITERS + 1),
            pltpu.VMEM((rows, layers, SUB, LANES), f32),
            pltpu.VMEM((rows, layers, SUB, LANES), f32),
            pltpu.VMEM((rows, layers - 1, SUB, LANES), f32),
            pltpu.VMEM((rows, SUB, LANES), f32),
            pltpu.VMEM((len(PAIRS), SUB, LANES), f32),
            pltpu.VMEM((slots, LANES), f32),
            pltpu.VMEM((max(inner_group - 1, 1), slots, LANES), f32),
            pltpu.VMEM((slots, LANES), f32),
            pltpu.VMEM((max(outer_group - 1, 1), slots, LANES), f32),
            pltpu.SemaphoreType.DMA((rows // SUB, len(folded))),
            pltpu.SemaphoreType.DMA((ITERS, 2, REACH)),
            pltpu.SemaphoreType.DMA((ITERS, 2, REACH)),
            pltpu.SemaphoreType.DMA((max(inner_group - 1, 1),)),
            pltpu.SemaphoreType.DMA((max(inner_group - 1, 1),)),
            pltpu.SemaphoreType.DMA((max(outer_group - 1, 1),)),
            pltpu.SemaphoreType.DMA((max(outer_group - 1, 1),)),
        ],
        compiler_params=pltpu.CompilerParams(
            collective_id=0, has_side_effects=True, vmem_limit_bytes=VMEM_BYTES - room
        ),
    )(*folded)
    return tuple(unfold(a, rows, cols) for a in outs)


def solution(mesh):
    return jax.shard_map(
        functools.partial(body, mesh.shape["flow"]),
        mesh=mesh,
        in_specs=(
            P(None, None, "flow", None),
            P("flow", None),
            P("flow", None),
            P("flow", None),
            P(None, "flow", None),
            P("flow", None),
            P("flow", None),
        ),
        out_specs=(P(None, None, "flow", None), P(None, None, "flow", None)),
        check_vma=False,
    )
```
